32 devices in a mesh: groups: 2 (over y), img: 8 (over z, x), sub: 2 (over core).
Axes of the slice: x: 2, y: 2, z: 4, core: 2. Of those that a mesh axis runs over, the one named last changes fastest.
Arguments:
- feats: bfloat16 [16, 128, 256], P(('groups', 'img')), parts along dimension 0
- grad_msg: bfloat16 [16, 128, 256], P(('groups', 'img'), None, 'sub'), parts along dimension 0, may hold values from -6 to 6
- w_qk: bfloat16 [256, 256], P(None, 'sub'), may hold values from -0.375 to 0.375
- w_v: bfloat16 [256, 256], P(None, 'sub'), may hold values from -0.375 to 0.375
- pair_slots: int32 [16, 4, 2], P(('groups', 'img')), parts along dimension 0, may hold values from -1 to 7, as said below
- counts: int32 [16], P(('groups', 'img')), parts along dimension 0, may hold values from 32 to 128, as said below
Outputs:
- grad_feats: bfloat16 [16, 128, 256], P(('groups', 'img'), None, 'sub'), parts along dimension 0
- grad_weights: float32 [4, 256, 256], P('groups', 'img', 'sub'), parts along dimension 0
The draws below stay inside these ranges and needn't reach their ends.
There are 2 independent parts, one for each index of `groups`. The reference program is written for one: setup_inputs(seed, part) draws one part's arguments, and reference() takes and returns one part's arrays. A program takes and returns all parts, laid end to end along the dimension named above; an argument that names none is the same for every part. Nothing has to cross between parts.
Inputs may be any that keep to these rules, and one draw needn't show every extreme that they name: `pair_slots`: row o lists the pairs owned by index o of img: (i, j) with i != j first, its remaining slots -1; 9 pairs in all; some owner lists exactly 4 pairs. `counts`: some image has all 128 keypoints.
All inputs are finite; a program needn't handle non-finite values.
Results may differ from the reference program's by a relative error of at most 0.012.
Values may be sent and summed in bfloat16 or wider, within the bound.
A program may use at most 64 MiB of HBM per device.

```python
import jax
import jax.numpy as jnp
from jax import lax

D = 256
HEAD_DIM = 64
KP = 128
PMAX = 4
IMAGES = 8
PAIRS = 9


def draw_feats(key, part):
    base_key = jax.random.fold_in(jax.random.fold_in(key, 3), 0)
    values = jax.random.normal(base_key, (IMAGES, KP, D), jnp.float32)
    return values.astype(jnp.bfloat16)


def draw_counts(key, part):
    size_key, full_key = jax.random.split(jax.random.fold_in(key, 5))
    sizes = jax.random.randint(size_key, (IMAGES,), KP // 4, KP + 1)
    fullest = jax.random.randint(full_key, (), 0, IMAGES)
    return sizes.at[fullest].set(KP).astype(jnp.int32)


def draw_pair_slots(key, part):
    keys = jax.random.split(jax.random.fold_in(key, 7), 5)
    left = jax.random.randint(keys[0], (PAIRS,), 0, IMAGES)
    right = (left + jax.random.randint(keys[1], (PAIRS,), 1, IMAGES)) % IMAGES
    busy = jax.random.randint(keys[2], (), 0, IMAGES)
    others = (jnp.arange((IMAGES - 1) * PMAX, dtype=jnp.int32) // PMAX + busy + 1) % IMAGES
    others = jax.random.permutation(keys[3], others)[:PAIRS - PMAX]
    owner = jnp.concatenate([jnp.full((PMAX,), busy, jnp.int32), others.astype(jnp.int32)])
    owner = jax.random.permutation(keys[4], owner)
    same = owner[:, None] == owner[None, :]
    earlier = jnp.arange(PAIRS)[None, :] < jnp.arange(PAIRS)[:, None]
    slot = jnp.sum((same & earlier).astype(jnp.int32), axis=1)
    table = jnp.full((IMAGES * PMAX, 2), -1, jnp.int32)
    table = table.at[owner * PMAX + slot].set(jnp.stack([left, right], axis=1).astype(jnp.int32))
    return table.reshape(IMAGES, PMAX, 2)


def block_scale(rng, shape, cuts, least, high):
    loudness = 1.0
    for position, shards_of in cuts:
        draws = jax.random.uniform(jax.random.fold_in(jax.random.fold_in(rng, 6), position), (shards_of,), jnp.float32, least / len(cuts), high / len(cuts))
        loudness = loudness * jnp.repeat(jnp.exp(draws), shape[position] // shards_of).reshape((-1,) + (1,) * (len(shape) - 1 - position))
    return loudness


def gaussian(stream_key, shape, scale, bound, cuts=(), kind=jnp.bfloat16):
    result = scale * jax.random.normal(stream_key, shape, jnp.float32)
    if cuts:
        result = result * block_scale(stream_key, shape, cuts, -0.22, 0.18)
    return jnp.clip(result, -bound, bound).astype(kind)


def setup_inputs(seed: int = 0, part: int = 0) -> dict:
    streams_of = jax.random.split(jax.random.key(seed), 7)
    part_keys = jax.random.split(jax.random.fold_in(streams_of[6], part), 7)
    feats = draw_feats(jax.random.fold_in(jax.random.fold_in(streams_of[6], part), 71), part)
    grad_msg = gaussian(part_keys[1], (IMAGES, KP, D), 1.0, 6.0, ((0, 8), (2, 2)))
    w_qk = gaussian(streams_of[2], (D, D), D ** -0.5, 0.375, ((1, 2),))
    w_v = gaussian(streams_of[3], (D, D), D ** -0.5, 0.375, ((1, 2),))
    pair_slots = draw_pair_slots(jax.random.fold_in(jax.random.fold_in(streams_of[6], part), 71), part)
    counts = draw_counts(jax.random.fold_in(jax.random.fold_in(streams_of[6], part), 71), part)
    return dict(feats=feats, grad_msg=grad_msg, w_qk=w_qk, w_v=w_v, pair_slots=pair_slots, counts=counts)


NEG_FILL = -1.0e30


def contract(left, right, left_dim, right_dim):
    return lax.dot_general(left, right, (((left_dim,), (right_dim,)), ((), ())), preferred_element_type=jnp.float32)


def normalize(scores, axis):
    top = jnp.max(scores, axis=axis, keepdims=True)
    weights = jnp.exp(scores - top)
    return weights / jnp.sum(weights, axis=axis, keepdims=True)


def head_backward(parts, scale):
    q_left, v_left, g_left, q_right, v_right, g_right, m_left, m_right = parts
    scores = contract(q_left, q_right, 1, 1) * scale
    row_probs = normalize(jnp.where(m_right[None, :] > 0, scores, NEG_FILL), 1)
    col_probs = normalize(jnp.where(m_left[:, None] > 0, scores, NEG_FILL), 0)
    gm_left = g_left * m_left[:, None]
    gm_right = g_right * m_right[:, None]
    row_low = row_probs.astype(jnp.bfloat16)
    col_low = col_probs.astype(jnp.bfloat16)
    dv_right = contract(row_low, gm_left, 0, 0)
    dv_left = contract(col_low, gm_right, 1, 0)
    drow = contract(gm_left, v_right, 1, 1)
    dcol = contract(v_left, gm_right, 1, 1)
    dscore = row_probs * (drow - jnp.sum(drow * row_probs, axis=1, keepdims=True))
    dscore = dscore + col_probs * (dcol - jnp.sum(dcol * col_probs, axis=0, keepdims=True))
    dscore_low = (dscore * scale).astype(jnp.bfloat16)
    dq_left = contract(dscore_low, q_right, 1, 0)
    dq_right = contract(dscore_low, q_left, 0, 0)
    return dq_left, dv_left, dq_right, dv_right


def slot_backward(block, mask):
    width = block.shape[-1] // 3
    local_heads = width // HEAD_DIM
    rows = block.shape[1]

    def heads_first(part):
        return part.reshape(rows, local_heads, HEAD_DIM).transpose(1, 0, 2)

    pieces = tuple(heads_first(block[side, :, kind * width:(kind + 1) * width]) for side in range(2) for kind in range(3))

    def one_head(item):
        return head_backward(item + (mask[0], mask[1]), HEAD_DIM ** -0.5)

    dq_left, dv_left, dq_right, dv_right = lax.map(one_head, pieces)

    def heads_last(part):
        return part.transpose(1, 0, 2).reshape(rows, width)

    left = jnp.concatenate([heads_last(dq_left), heads_last(dv_left)], axis=1)
    right = jnp.concatenate([heads_last(dq_right), heads_last(dv_right)], axis=1)
    return jnp.stack([left, right]).astype(jnp.bfloat16)


def reference(feats, grad_msg, w_qk, w_v, pair_slots, counts):
    images, rows, width = feats.shape
    flat_feats = feats.reshape(images * rows, width)
    query_keys = jnp.dot(flat_feats, w_qk, preferred_element_type=jnp.float32).astype(jnp.bfloat16).reshape(images, rows, width)
    values = jnp.dot(flat_feats, w_v, preferred_element_type=jnp.float32).astype(jnp.bfloat16).reshape(images, rows, width)
    packed = jnp.concatenate([query_keys, values, grad_msg], axis=2)
    flat = pair_slots.reshape(-1, 2)
    live = flat[:, 0] >= 0
    order = jnp.cumsum(live.astype(jnp.int32)) - 1
    target = jnp.where(live, order, PAIRS).astype(jnp.int32)
    chosen = jnp.zeros((PAIRS + 1, 2), jnp.int32).at[target].set(flat)[:PAIRS]
    positions = jnp.arange(rows, dtype=jnp.int32)

    def step(totals, pair):
        left = pair[0]
        right = pair[1]
        block = jnp.stack([packed[left], packed[right]])
        mask = jnp.stack([positions < counts[left], positions < counts[right]]).astype(jnp.bfloat16)
        grads = slot_backward(block, mask).astype(jnp.float32)
        totals = totals.at[left].add(grads[0])
        totals = totals.at[right].add(grads[1])
        return totals, None

    totals, _ = lax.scan(step, jnp.zeros((images, rows, 2 * width), jnp.float32), chosen)
    grad_qk = totals[:, :, :width].astype(jnp.bfloat16).reshape(-1, width)
    grad_v = totals[:, :, width:].astype(jnp.bfloat16).reshape(-1, width)
    grad_feats = jnp.dot(grad_qk, w_qk.T, preferred_element_type=jnp.float32) + jnp.dot(grad_v, w_v.T, preferred_element_type=jnp.float32)
    grad_feats = grad_feats.astype(jnp.bfloat16).reshape(images, rows, width)
    grad_weights = jnp.stack([contract(flat_feats, grad_qk, 0, 0), contract(flat_feats, grad_v, 0, 0)])
    return grad_feats, grad_weights
```

```python
import functools

import jax
import jax.numpy as jnp
from jax import lax
from jax.experimental import pallas as pl
from jax.experimental.pallas import tpu as pltpu
from jax.sharding import PartitionSpec as P

HEAD_DIM = 64
NEG_FILL = -1e30
TABLE = 128
MESH = pl.DeviceIdType.MESH
ANY = pl.BlockSpec(memory_space=pl.ANY)
VMEM = pl.BlockSpec(memory_space=pltpu.VMEM)
SMEM = pl.BlockSpec(memory_space=pltpu.SMEM)


def contract(left, right, left_dim, right_dim):
    return lax.dot_general(
        left, right, (((left_dim,), (right_dim,)), ((), ())), preferred_element_type=jnp.float32
    )


def greet(n, me, sub):
    barrier = pltpu.get_barrier_semaphore()
    for d in range(1, n):
        pl.semaphore_signal(
            barrier, inc=1, device_id={"img": lax.rem(me + d, n)}, device_id_type=MESH
        )
    pl.semaphore_signal(barrier, inc=1, device_id={"sub": 1 - sub}, device_id_type=MESH)
    return barrier


def gather_kernel(
    n, feats, grad, table, all_feats, all_grad, all_table,
    local_sem, zf_send, zg_send, xf_send, xg_send, c_send, t_send, f_recv, g_recv, c_recv, t_recv,
):
    me = lax.axis_index("img")
    sub = lax.axis_index("sub")
    columns = n // 2
    z, x = me // 2, lax.rem(me, 2)
    half = feats.shape[1] // 2
    mine = pl.ds(pl.multiple_of(sub * half, half), half)
    other = pl.ds(pl.multiple_of((1 - sub) * half, half), half)

    barrier = greet(n, me, sub)
    own = [
        pltpu.make_async_copy(feats.at[0], all_feats.at[me], local_sem.at[0]),
        pltpu.make_async_copy(grad.at[0], all_grad.at[me], local_sem.at[1]),
        pltpu.make_async_copy(table.at[0], all_table.at[me], local_sem.at[2]),
    ]
    for copy in own:
        copy.start()
    pl.semaphore_wait(barrier, n)

    def push(src, dst, send, recv, device):
        copy = pltpu.make_async_remote_copy(
            src_ref=src, dst_ref=dst, send_sem=send, recv_sem=recv,
            device_id=device, device_id_type=MESH,
        )
        return copy

    def feats_copy(src, block, send, device):
        return push(src, all_feats.at[block, mine], send, f_recv.at[block], device)

    def grad_copy(src, block, send, device):
        return push(src, all_grad.at[block], send, g_recv.at[block], device)

    def core_copy(block, rows):
        return push(
            all_feats.at[block, rows], all_feats.at[block, rows], c_send.at[block],
            c_recv.at[block], {"sub": 1 - sub},
        )

    across = {"img": z * 2 + 1 - x}
    sent = []

    def go(copy):
        copy.start()
        sent.append(copy)

    for d in range(1, n):
        go(push(
            table.at[0], all_table.at[me], t_send.at[d], t_recv.at[me],
            {"img": lax.rem(me + d, n)},
        ))
    go(feats_copy(feats.at[0, mine], me, xf_send.at[0], across))
    go(grad_copy(grad.at[0], me, xg_send.at[0], across))
    for d in range(1, columns):
        target = {"img": lax.rem(z + d, columns) * 2 + x}
        go(feats_copy(feats.at[0, mine], me, zf_send.at[d], target))
        go(grad_copy(grad.at[0], me, zg_send.at[d], target))
    for d in range(1, columns):
        block = lax.rem(z + columns - d, columns) * 2 + x
        feats_copy(all_feats.at[block, mine], block, xf_send.at[d], across).wait_recv()
        go(feats_copy(all_feats.at[block, mine], block, xf_send.at[d], across))
        go(core_copy(block, mine))
        grad_copy(all_grad.at[block], block, xg_send.at[d], across).wait_recv()
        go(grad_copy(all_grad.at[block], block, xg_send.at[d], across))
    for d in range(columns):
        block = lax.rem(z + columns - d, columns) * 2 + 1 - x
        feats_copy(all_feats.at[block, mine], block, xf_send.at[d], across).wait_recv()
        go(core_copy(block, mine))
    for d in range(columns):
        block = lax.rem(z + columns - d, columns) * 2 + 1 - x
        grad_copy(all_grad.at[block], block, xg_send.at[d], across).wait_recv()
    for d in range(1, n):
        block = lax.rem(me + d, n)
        core_copy(block, other).wait_recv()
        push(
            table.at[0], all_table.at[block], t_send.at[d], t_recv.at[block], {"img": block}
        ).wait_recv()
    for copy in own:
        copy.wait()
    for copy in sent:
        copy.wait_send()


def gather(n, feats, grad, table):
    rows, depth = feats.shape[1:]
    width = grad.shape[2]
    dma = pltpu.SemaphoreType.DMA
    return pl.pallas_call(
        functools.partial(gather_kernel, n),
        out_shape=(
            jax.ShapeDtypeStruct((n, rows, depth), feats.dtype),
            jax.ShapeDtypeStruct((n, rows, width), grad.dtype),
            jax.ShapeDtypeStruct((n, 1, TABLE), table.dtype),
        ),
        in_specs=[ANY] * 3,
        out_specs=(ANY,) * 3,
        scratch_shapes=[
            dma((3,)), dma((n // 2,)), dma((n // 2,)), dma((n // 2,)), dma((n // 2,)),
            dma((n,)), dma((n,)), dma((n,)), dma((n,)), dma((n,)), dma((n,)),
        ],
        compiler_params=pltpu.CompilerParams(collective_id=0, has_side_effects=True),
        name="gather",
    )(feats, grad, table)


def pair_kernel(slots, table, feats, grad, w_qk, w_v, out, acc, peers):
    me = lax.axis_index("img")
    n, rows, _ = feats.shape
    width = w_qk.shape[1]
    heads = width // HEAD_DIM
    scale = HEAD_DIM ** (-0.5)

    def scan(s, count):
        owner, k = s // slots, lax.rem(s, slots)
        i, j = table[owner, 0, 2 * k], table[owner, 0, 2 * k + 1]
        hit = (i >= 0) & ((i == me) | (j == me))
        peers[count] = jnp.where(i == me, j, i)
        return count + hit.astype(jnp.int32)

    total = lax.fori_loop(0, n * slots, scan, jnp.int32(0), unroll=8)

    def project(which):
        f = feats[which]
        q = jnp.dot(f, w_qk[...], preferred_element_type=jnp.float32).astype(jnp.bfloat16)
        v = jnp.dot(f, w_v[...], preferred_element_type=jnp.float32).astype(jnp.bfloat16)
        live = lax.broadcasted_iota(jnp.int32, (rows, width), 0) < table[which, 0, 2 * slots]
        g = jnp.where(live, grad[which], jnp.zeros((), jnp.bfloat16))
        return q, v, g

    def stack(part):
        head = lax.broadcasted_iota(jnp.int32, part.shape, 1) // HEAD_DIM
        zero = jnp.zeros((), part.dtype)
        return jnp.concatenate([jnp.where(head == h, part, zero) for h in range(heads)], axis=0)

    q_own, v_own, g_own = project(me)
    count_own = table[me, 0, 2 * slots]
    row_live = lax.broadcasted_iota(jnp.int32, (rows, heads * rows), 0) < count_own
    acc[...] = jnp.zeros_like(acc)

    def step(t, carry):
        peer = peers[t]
        q_peer, v_peer, g_peer = (stack(part) for part in project(peer))
        count_peer = table[peer, 0, 2 * slots]
        scores = contract(q_own, q_peer, 1, 1) * scale
        drow = contract(g_own, v_peer, 1, 1)
        dcol = contract(v_own, g_peer, 1, 1)
        masked = jnp.where(row_live, scores, NEG_FILL)
        e = jnp.exp(masked - jnp.max(masked, axis=0, keepdims=True))
        col = e * (1.0 / jnp.sum(e, axis=0, keepdims=True))
        dcol = col * (dcol - jnp.sum(dcol * col, axis=0, keepdims=True))
        col_live = lax.broadcasted_iota(jnp.int32, (rows, rows), 1) < count_peer
        pieces = []
        for h in range(heads):
            part = slice(h * rows, (h + 1) * rows)
            masked = jnp.where(col_live, scores[:, part], NEG_FILL)
            e = jnp.exp(masked - jnp.max(masked, axis=1, keepdims=True))
            row = e * (1.0 / jnp.sum(e, axis=1, keepdims=True))
            d = drow[:, part]
            d = row * (d - jnp.sum(d * row, axis=1, keepdims=True))
            pieces.append(((d + dcol[:, part]) * scale).astype(jnp.bfloat16))
        dscore = jnp.concatenate(pieces, axis=1)
        acc[:, :width] += contract(dscore, q_peer, 1, 0)
        acc[:, width:] += contract(col.astype(jnp.bfloat16), g_peer, 1, 0)
        return carry

    lax.fori_loop(0, total, step, 0)
    out[...] = acc[...].astype(out.dtype)


def pair_sides(slots, table, feats, grad, w_qk, w_v):
    n, rows, _ = feats.shape
    width = w_qk.shape[1]
    return pl.pallas_call(
        functools.partial(pair_kernel, slots),
        out_shape=jax.ShapeDtypeStruct((rows, 2 * width), jnp.bfloat16),
        in_specs=[SMEM, VMEM, VMEM, VMEM, VMEM],
        out_specs=VMEM,
        scratch_shapes=[
            pltpu.VMEM((rows, 2 * width), jnp.float32),
            pltpu.SMEM((n * slots + 1,), jnp.int32),
        ],
        compiler_params=pltpu.CompilerParams(vmem_limit_bytes=40 * 1024 * 1024),
        name="pairs",
    )(table, feats, grad, w_qk, w_v)


def reduce_kernel(
    n, feats, both, w_qk, w_v, grad_feats, grad_weights,
    terms, outgoing, arrived, term, term_in, w_send, w_recv, t_send, t_recv,
):
    me = lax.axis_index("img")
    sub = lax.axis_index("sub")
    width = w_qk.shape[1]
    share = terms.shape[1]
    barrier = greet(n, me, sub)
    products = contract(feats[0], both[...], 0, 0)
    for c in range(n):
        piece = products[c * share : (c + 1) * share]
        terms[c] = piece
        outgoing[c] = piece.astype(jnp.bfloat16)
    pl.semaphore_wait(barrier, n)
    sent = []
    for d in range(1, n):
        target = lax.rem(me + d, n)
        copy = pltpu.make_async_remote_copy(
            src_ref=outgoing.at[target], dst_ref=arrived.at[n - d],
            send_sem=w_send.at[d], recv_sem=w_recv.at[n - d],
            device_id={"img": target}, device_id_type=MESH,
        )
        copy.start()
        sent.append(copy)
    for c in range(2):
        rows = slice(c * width, (c + 1) * width)
        term[c] = contract(both[:, :width], w_qk[rows], 1, 1) + contract(
            both[:, width:], w_v[rows], 1, 1
        )
    swap = pltpu.make_async_remote_copy(
        src_ref=term.at[1 - sub], dst_ref=term_in,
        send_sem=t_send.at[0], recv_sem=t_recv.at[0],
        device_id={"sub": 1 - sub}, device_id_type=MESH,
    )
    swap.start()
    swap.wait_recv()
    grad_feats[0] = (term[sub] + term_in[...]).astype(grad_feats.dtype)
    total = terms[me]
    for copy in reversed(sent):
        copy.wait_recv()
    for d in range(1, n):
        total = total + arrived[d].astype(jnp.float32)
    grad_weights[0] = total[:, :width]
    grad_weights[1] = total[:, width:]
    swap.wait_send()
    for copy in sent:
        copy.wait_send()


def reduce_terms(n, feats, both, w_qk, w_v):
    rows, depth = feats.shape[1:]
    width = w_qk.shape[1]
    share = depth // n
    dma = pltpu.SemaphoreType.DMA
    return pl.pallas_call(
        functools.partial(reduce_kernel, n),
        out_shape=(
            jax.ShapeDtypeStruct((1, rows, width), jnp.bfloat16),
            jax.ShapeDtypeStruct((2, share, width), jnp.float32),
        ),
        in_specs=[VMEM] * 4,
        out_specs=(VMEM,) * 2,
        scratch_shapes=[
            pltpu.VMEM((n, share, 2 * width), jnp.float32),
            pltpu.VMEM((n, share, 2 * width), jnp.bfloat16),
            pltpu.VMEM((n, share, 2 * width), jnp.bfloat16),
            pltpu.VMEM((2, rows, width), jnp.float32),
            pltpu.VMEM((rows, width), jnp.float32),
            dma((n,)), dma((n,)), dma((1,)), dma((1,)),
        ],
        compiler_params=pltpu.CompilerParams(collective_id=1, has_side_effects=True),
        name="reduce",
    )(feats, both, w_qk, w_v)


def local(feats, grad_msg, w_qk, w_v, pair_slots, counts):
    n = lax.axis_size("img")
    slots = pair_slots.shape[1]
    table = jnp.concatenate([pair_slots.reshape(-1), counts])
    table = jnp.pad(table, (0, TABLE - table.shape[0])).reshape(1, 1, TABLE)
    all_feats, all_grad, all_table = gather(n, feats, grad_msg, table)
    both = pair_sides(slots, all_table, all_feats, all_grad, w_qk, w_v)
    return reduce_terms(n, feats, both, w_qk, w_v)


def solution(mesh):
    in_specs = (
        P(("groups", "img"), None, None),
        P(("groups", "img"), None, "sub"),
        P(None, "sub"),
        P(None, "sub"),
        P(("groups", "img"), None, None),
        P(("groups", "img")),
    )
    out_specs = (P(("groups", "img"), None, "sub"), P("groups", "img", "sub"))
    return jax.shard_map(local, mesh=mesh, in_specs=in_specs, out_specs=out_specs, check_vma=False)
```

```python
import functools

import jax
import jax.numpy as jnp
from jax import lax
from jax.experimental import pallas as pl
from jax.experimental.pallas import tpu as pltpu
from jax.sharding import PartitionSpec as P

HEAD_DIM = 64
NEG_FILL = -1e30
LANES = 128
MESH = pl.DeviceIdType.MESH
ANY = pl.BlockSpec(memory_space=pl.ANY)
VMEM = pl.BlockSpec(memory_space=pltpu.VMEM)
SMEM = pl.BlockSpec(memory_space=pltpu.SMEM)


def contract(left, right, left_dim, right_dim):
    return lax.dot_general(
        left, right, (((left_dim,), (right_dim,)), ((), ())), preferred_element_type=jnp.float32
    )


def loop(low, high, body):
    if high - low <= 8:
        for d in range(low, high):
            body(d)
    else:

        def step(d, carry):
            body(d)
            return carry

        lax.fori_loop(low, high, step, 0)


def kernel(
    n, feats, grad, w_qk_in, w_v_in, pairs, counts, grad_feats, grad_weights,
    all_feats, all_grad, table, w_qk, w_v, acc, terms, outgoing, arrived, term, term_in,
    local_sem, zf_send, zg_send, xf_send, xg_send, c_send, t_send, f_recv, g_recv, c_recv, t_recv,
    w_send, w_recv, s_send, s_recv,
):
    me = lax.axis_index("img")
    sub = lax.axis_index("sub")
    columns = n // 2
    z, x = me // 2, lax.rem(me, 2)
    rows = feats.shape[1]
    half = rows // 2
    width = w_qk.shape[1]
    heads = width // HEAD_DIM
    scale = HEAD_DIM ** (-0.5)
    share = terms.shape[1]
    mine = pl.ds(pl.multiple_of(sub * half, half), half)
    other = pl.ds(pl.multiple_of((1 - sub) * half, half), half)
    across = {"img": z * 2 + 1 - x}
    partner = {"sub": 1 - sub}

    barrier = pltpu.get_barrier_semaphore()
    loop(1, n, lambda d: pl.semaphore_signal(
        barrier, inc=1, device_id={"img": lax.rem(me + d, n)}, device_id_type=MESH
    ))
    pl.semaphore_signal(barrier, inc=1, device_id=partner, device_id_type=MESH)

    own = [
        pltpu.make_async_copy(feats.at[0], all_feats.at[me], local_sem.at[0]),
        pltpu.make_async_copy(w_qk_in, w_qk, local_sem.at[1]),
        pltpu.make_async_copy(w_v_in, w_v, local_sem.at[2]),
        pltpu.make_async_copy(grad.at[0], all_grad.at[me], local_sem.at[3]),
    ]
    for copy in own:
        copy.start()

    lane = lax.broadcasted_iota(jnp.int32, (1, LANES), 1)
    codes = jnp.full((1, LANES), -1, jnp.int32)
    for k in range(pairs.shape[1]):
        left, right = pairs[0, k, 0], pairs[0, k, 1]
        codes = jnp.where(lane == k, jnp.where(left >= 0, left * n + right, -1), codes)
    table[me] = jnp.concatenate([codes, jnp.full((1, LANES), counts[0], jnp.int32)], axis=0)
    pl.semaphore_wait(barrier, n)

    def push(src, dst, send, recv, device):
        return pltpu.make_async_remote_copy(
            src_ref=src, dst_ref=dst, send_sem=send, recv_sem=recv,
            device_id=device, device_id_type=MESH,
        )

    def column(d):
        return lax.rem(z + columns - d, columns) * 2

    def feats_x(block, d):
        return push(
            all_feats.at[block, mine], all_feats.at[block, mine], xf_send.at[d], f_recv.at[block], across
        )

    def grad_x(block, d):
        return push(all_grad.at[block], all_grad.at[block], xg_send.at[d], g_recv.at[block], across)

    def own_feats(send, device):
        return push(feats.at[0, mine], all_feats.at[me, mine], send, f_recv.at[me], device)

    def own_grad(send, device):
        return push(grad.at[0], all_grad.at[me], send, g_recv.at[me], device)

    def column_target(d):
        return {"img": lax.rem(z + d, columns) * 2 + x}

    def core(block, half_rows):
        return push(
            all_feats.at[block, half_rows], all_feats.at[block, half_rows], c_send.at[block],
            c_recv.at[block], partner,
        )

    def table_copy(d):
        return push(
            table.at[me], table.at[me], t_send.at[d], t_recv.at[me], {"img": lax.rem(me + d, n)}
        )

    def table_wait(d):
        block = lax.rem(me + d, n)
        push(
            table.at[block], table.at[block], t_send.at[d], t_recv.at[block], {"img": block}
        ).wait_recv()

    loop(1, n, lambda d: table_copy(d).start())
    own_feats(xf_send.at[0], across).start()
    own_grad(xg_send.at[0], across).start()

    def send_column(d):
        own_feats(zf_send.at[d], column_target(d)).start()
        own_grad(zg_send.at[d], column_target(d)).start()

    loop(1, columns, send_column)

    def arrive_column(d):
        block = column(d) + x
        feats_x(block, d).wait_recv()
        feats_x(block, d).start()
        core(block, mine).start()
        grad_x(block, d).wait_recv()
        grad_x(block, d).start()

    def arrive_across(d):
        block = column(d) + 1 - x
        feats_x(block, d).wait_recv()
        core(block, mine).start()
        grad_x(block, d).wait_recv()

    for copy in own:
        copy.wait()

    row_ids = lax.broadcasted_iota(jnp.int32, (rows, width), 0)

    def project(which):
        f = all_feats[which]
        q = jnp.dot(f, w_qk[...], preferred_element_type=jnp.float32).astype(jnp.bfloat16)
        v = jnp.dot(f, w_v[...], preferred_element_type=jnp.float32).astype(jnp.bfloat16)
        count = table[which, 1:2, :]
        g = jnp.where(row_ids < count, all_grad[which], jnp.zeros((), jnp.bfloat16))
        return q, v, g, count

    def stack(part):
        head = lax.broadcasted_iota(jnp.int32, part.shape, 1) // HEAD_DIM
        zero = jnp.zeros((), part.dtype)
        return jnp.concatenate([jnp.where(head == h, part, zero) for h in range(heads)], axis=0)

    q_own, v_own, g_own, count_own = project(me)
    wide = (rows, heads * rows)
    row_live = lax.broadcasted_iota(jnp.int32, wide, 0) < jnp.concatenate([count_own] * heads, axis=1)
    acc[...] = jnp.zeros_like(acc)
    loop(1, n, table_wait)

    def work(peer):
        core(peer, other).wait_recv()
        q_peer, v_peer, g_peer, count_peer = project(peer)
        q_peer, v_peer, g_peer = stack(q_peer), stack(v_peer), stack(g_peer)
        listed = table[:, 0, :]
        hits = (listed == me * n + peer) | (listed == peer * n + me)
        times = jnp.sum(hits.astype(jnp.float32), keepdims=True)
        scores = contract(q_own, q_peer, 1, 1) * scale
        drow = contract(g_own, v_peer, 1, 1)
        dcol = contract(v_own, g_peer, 1, 1)
        masked = jnp.where(row_live, scores, NEG_FILL)
        e = jnp.exp(masked - jnp.max(masked, axis=0, keepdims=True))
        col = e * (1.0 / jnp.sum(e, axis=0, keepdims=True))
        dcol = col * (dcol - jnp.sum(dcol * col, axis=0, keepdims=True))
        col_live = lax.broadcasted_iota(jnp.int32, (rows, rows), 1) < count_peer
        pieces = []
        for h in range(heads):
            part = slice(h * rows, (h + 1) * rows)
            masked = jnp.where(col_live, scores[:, part], NEG_FILL)
            e = jnp.exp(masked - jnp.max(masked, axis=1, keepdims=True))
            row = e * (1.0 / jnp.sum(e, axis=1, keepdims=True))
            d = drow[:, part]
            d = row * (d - jnp.sum(d * row, axis=1, keepdims=True))
            pieces.append(((d + dcol[:, part]) * scale).astype(jnp.bfloat16))
        dscore = jnp.concatenate(pieces, axis=1)
        acc[:, :width] += times * contract(dscore, q_peer, 1, 0)
        acc[:, width:] += times * contract(col.astype(jnp.bfloat16), g_peer, 1, 0)

    def next_column(d):
        arrive_column(d)
        work(column(d - 1) + x)

    def next_across(d):
        arrive_across(d)
        work(column(d - 1) + 1 - x)

    arrive_across(0)
    arrive_column(1)
    work(column(0) + 1 - x)
    loop(2, columns, next_column)
    arrive_across(1)
    work(column(columns - 1) + x)
    loop(2, columns, next_across)
    work(column(columns - 1) + 1 - x)

    both = acc[...].astype(jnp.bfloat16)
    products = contract(all_feats[me], both, 0, 0)
    for c in range(n):
        piece = products[c * share : (c + 1) * share]
        terms[c] = piece
        outgoing[c] = piece.astype(jnp.bfloat16)

    def weight_copy(d):
        target = lax.rem(me + d, n)
        return push(
            outgoing.at[target], arrived.at[n - d], w_send.at[d], w_recv.at[n - d], {"img": target}
        )

    loop(1, n, lambda d: weight_copy(d).start())
    for c in range(2):
        part = slice(c * width, (c + 1) * width)
        term[c] = contract(both[:, :width], w_qk[part], 1, 1) + contract(
            both[:, width:], w_v[part], 1, 1
        )
    swap = push(term.at[1 - sub], term_in, s_send.at[0], s_recv.at[0], partner)
    swap.start()
    swap.wait_recv()
    grad_feats[0] = (term[sub] + term_in[...]).astype(grad_feats.dtype)

    total = terms[me]
    loop(1, n, lambda d: weight_copy(d).wait_recv())
    for d in range(1, n):
        total = total + arrived[d].astype(jnp.float32)
    grad_weights[0] = total[:, :width]
    grad_weights[1] = total[:, width:]

    swap.wait_send()
    loop(1, n, lambda d: weight_copy(d).wait_send())
    loop(1, n, lambda d: table_copy(d).wait_send())
    own_feats(xf_send.at[0], across).wait_send()
    own_grad(xg_send.at[0], across).wait_send()

    def sent_column(d):
        own_feats(zf_send.at[d], column_target(d)).wait_send()
        own_grad(zg_send.at[d], column_target(d)).wait_send()
        feats_x(column(d) + x, d).wait_send()
        grad_x(column(d) + x, d).wait_send()

    loop(1, columns, sent_column)
    loop(1, n, lambda d: core(lax.rem(me + d, n), mine).wait_send())


def local(feats, grad_msg, w_qk, w_v, pair_slots, counts):
    n = lax.axis_size("img")
    rows, depth = feats.shape[1:]
    width = w_qk.shape[1]
    share = depth // n
    low, full = jnp.bfloat16, jnp.float32
    vmem = pltpu.VMEM
    dma = pltpu.SemaphoreType.DMA
    return pl.pallas_call(
        functools.partial(kernel, n),
        out_shape=(
            jax.ShapeDtypeStruct((1, rows, width), low),
            jax.ShapeDtypeStruct((2, share, width), full),
        ),
        in_specs=[ANY] * 4 + [SMEM] * 2,
        out_specs=(VMEM,) * 2,
        scratch_shapes=[
            vmem((n, rows, depth), low),
            vmem((n, rows, width), low),
            vmem((n, 2, LANES), jnp.int32),
            vmem((depth, width), low),
            vmem((depth, width), low),
            vmem((rows, 2 * width), full),
            vmem((n, share, 2 * width), full),
            vmem((n, share, 2 * width), low),
            vmem((n, share, 2 * width), low),
            vmem((2, rows, width), full),
            vmem((rows, width), full),
            dma((4,)),
            dma((n // 2,)), dma((n // 2,)), dma((n // 2,)), dma((n // 2,)),
            dma((n,)), dma((n,)), dma((n,)), dma((n,)), dma((n,)), dma((n,)),
            dma((n,)), dma((n,)), dma((1,)), dma((1,)),
        ],
        compiler_params=pltpu.CompilerParams(
            collective_id=0, has_side_effects=True, vmem_limit_bytes=40 * 1024 * 1024
        ),
        name="backward",
    )(feats, grad_msg, w_qk, w_v, pair_slots, counts)


def solution(mesh):
    in_specs = (
        P(("groups", "img"), None, None),
        P(("groups", "img"), None, "sub"),
        P(None, "sub"),
        P(None, "sub"),
        P(("groups", "img"), None, None),
        P(("groups", "img")),
    )
    out_specs = (P(("groups", "img"), None, "sub"), P("groups", "img", "sub"))
    return jax.shard_map(local, mesh=mesh, in_specs=in_specs, out_specs=out_specs, check_vma=False)
```

```python
import functools

import jax
import jax.numpy as jnp
from jax import lax
from jax.experimental import pallas as pl
from jax.experimental.pallas import tpu as pltpu
from jax.sharding import PartitionSpec as P

HEAD_DIM = 64
NEG_FILL = -1e30
LANES = 128
MESH = pl.DeviceIdType.MESH
HBM = pl.BlockSpec(memory_space=pltpu.HBM)
VMEM = pl.BlockSpec(memory_space=pltpu.VMEM)
SMEM = pl.BlockSpec(memory_space=pltpu.SMEM)


def contract(left, right, left_dim, right_dim):
    return lax.dot_general(
        left, right, (((left_dim,), (right_dim,)), ((), ())), preferred_element_type=jnp.float32
    )


def loop(low, high, body):
    if high - low <= 8:
        for d in range(low, high):
            body(d)
    else:

        def step(d, carry):
            body(d)
            return carry

        lax.fori_loop(low, high, step, 0)


def kernel(
    n, feats, grad, w_qk_in, w_v_in, pairs, counts, grad_feats, grad_weights,
    all_feats, all_grad, table, w_qk, w_v, acc, terms, outgoing, arrived, term, term_in,
    local_sem, zf_send, zg_send, xf_send, xg_send, c_send, t_send, f_recv, g_recv, c_recv, t_recv,
    w_send, w_recv, s_send, s_recv,
):
    me = lax.axis_index("img")
    sub = lax.axis_index("sub")
    columns = n // 2
    z, x = me // 2, lax.rem(me, 2)
    rows = feats.shape[1]
    half = rows // 2
    width = w_qk.shape[1]
    heads = width // HEAD_DIM
    scale = HEAD_DIM ** (-0.5)
    share = terms.shape[1]
    mine = pl.ds(pl.multiple_of(sub * half, half), half)
    other = pl.ds(pl.multiple_of((1 - sub) * half, half), half)
    across = {"img": z * 2 + 1 - x}
    partner = {"sub": 1 - sub}

    barrier = pltpu.get_barrier_semaphore()
    loop(1, n, lambda d: pl.semaphore_signal(
        barrier, inc=1, device_id={"img": lax.rem(me + d, n)}, device_id_type=MESH
    ))
    pl.semaphore_signal(barrier, inc=1, device_id=partner, device_id_type=MESH)

    own = [
        pltpu.make_async_copy(feats.at[0], all_feats.at[me], local_sem.at[0]),
        pltpu.make_async_copy(w_qk_in, w_qk, local_sem.at[1]),
        pltpu.make_async_copy(w_v_in, w_v, local_sem.at[2]),
        pltpu.make_async_copy(grad.at[0], all_grad.at[me], local_sem.at[3]),
    ]
    for copy in own:
        copy.start()

    lane = lax.broadcasted_iota(jnp.int32, (1, LANES), 1)
    codes = jnp.full((1, LANES), -1, jnp.int32)
    for k in range(pairs.shape[2]):
        left, right = pairs[0, 0, k], pairs[0, 1, k]
        codes = jnp.where(lane == k, jnp.where(left >= 0, left * n + right, -1), codes)
    table[me] = jnp.concatenate([codes, jnp.full((1, LANES), counts[0], jnp.int32)], axis=0)
    pl.semaphore_wait(barrier, n)

    def push(src, dst, send, recv, device):
        return pltpu.make_async_remote_copy(
            src_ref=src, dst_ref=dst, send_sem=send, recv_sem=recv,
            device_id=device, device_id_type=MESH,
        )

    def column(d):
        meets, bit = z, 1
        while bit < columns:
            meets = meets + (d // bit % 2) * (bit - 2 * bit * (z // bit % 2))
            bit *= 2
        return meets * 2

    def feats_x(block, d):
        return push(
            all_feats.at[block, mine], all_feats.at[block, mine], xf_send.at[d], f_recv.at[block], across
        )

    def grad_x(block, d):
        return push(all_grad.at[block], all_grad.at[block], xg_send.at[d], g_recv.at[block], across)

    def own_feats(send, device):
        return push(feats.at[0, mine], all_feats.at[me, mine], send, f_recv.at[me], device)

    def own_grad(send, device):
        return push(grad.at[0], all_grad.at[me], send, g_recv.at[me], device)

    def column_target(d):
        return {"img": column(d) + x}

    def core(block, half_rows):
        return push(
            all_feats.at[block, half_rows], all_feats.at[block, half_rows], c_send.at[block],
            c_recv.at[block], partner,
        )

    def table_copy(d):
        return push(
            table.at[me], table.at[me], t_send.at[d], t_recv.at[me], {"img": lax.rem(me + d, n)}
        )

    def table_wait(d):
        block = lax.rem(me + d, n)
        push(
            table.at[block], table.at[block], t_send.at[d], t_recv.at[block], {"img": block}
        ).wait_recv()

    loop(1, n, lambda d: table_copy(d).start())
    own_feats(xf_send.at[0], across).start()
    own_grad(xg_send.at[0], across).start()

    def send_column(d):
        own_feats(zf_send.at[d], column_target(d)).start()
        own_grad(zg_send.at[d], column_target(d)).start()

    loop(1, columns, lambda d: send_column(d))

    def arrive_column(d):
        block = column(d) + x
        feats_x(block, d).wait_recv()
        feats_x(block, d).start()
        core(block, mine).start()
        grad_x(block, d).wait_recv()
        grad_x(block, d).start()

    def arrive_across(d):
        block = column(d) + 1 - x
        feats_x(block, d).wait_recv()
        core(block, mine).start()
        grad_x(block, d).wait_recv()

    for copy in own:
        copy.wait()

    row_ids = lax.broadcasted_iota(jnp.int32, (rows, width), 0)

    def project(which):
        f = all_feats[which]
        q = jnp.dot(f, w_qk[...], preferred_element_type=jnp.float32).astype(jnp.bfloat16)
        v = jnp.dot(f, w_v[...], preferred_element_type=jnp.float32).astype(jnp.bfloat16)
        count = table[which, 1:2, :]
        g = jnp.where(row_ids < count, all_grad[which], jnp.zeros((), jnp.bfloat16))
        return q, v, g, count

    def stack(part):
        head = lax.broadcasted_iota(jnp.int32, part.shape, 1) // HEAD_DIM
        zero = jnp.zeros((), part.dtype)
        return jnp.concatenate([jnp.where(head == h, part, zero) for h in range(heads)], axis=0)

    q_own, v_own, g_own, count_own = project(me)
    wide = (rows, heads * rows)
    row_live = lax.broadcasted_iota(jnp.int32, wide, 0) < jnp.concatenate([count_own] * heads, axis=1)
    acc[...] = jnp.zeros_like(acc)

    def work(peer):
        core(peer, other).wait_recv()
        q_peer, v_peer, g_peer, count_peer = project(peer)
        q_peer, v_peer, g_peer = stack(q_peer), stack(v_peer), stack(g_peer)
        listed = table[:, 0, :]
        hits = (listed == me * n + peer) | (listed == peer * n + me)
        times = jnp.sum(hits.astype(jnp.float32), keepdims=True)
        scores = contract(q_own, q_peer, 1, 1) * scale
        drow = contract(g_own, v_peer, 1, 1)
        dcol = contract(v_own, g_peer, 1, 1)
        masked = jnp.where(row_live, scores, NEG_FILL)
        e = jnp.exp(masked - jnp.max(masked, axis=0, keepdims=True))
        col = e * (1.0 / jnp.sum(e, axis=0, keepdims=True))
        dcol = col * (dcol - jnp.sum(dcol * col, axis=0, keepdims=True))
        col_live = lax.broadcasted_iota(jnp.int32, (rows, rows), 1) < count_peer
        pieces = []
        for h in range(heads):
            part = slice(h * rows, (h + 1) * rows)
            masked = jnp.where(col_live, scores[:, part], NEG_FILL)
            e = jnp.exp(masked - jnp.max(masked, axis=1, keepdims=True))
            row = e * (1.0 / jnp.sum(e, axis=1, keepdims=True))
            d = drow[:, part]
            d = row * (d - jnp.sum(d * row, axis=1, keepdims=True))
            pieces.append(((d + dcol[:, part]) * scale).astype(jnp.bfloat16))
        dscore = jnp.concatenate(pieces, axis=1)
        acc[:, :width] += times * contract(dscore, q_peer, 1, 0)
        acc[:, width:] += times * contract(col.astype(jnp.bfloat16), g_peer, 1, 0)

    def next_column(d):
        arrive_column(d)
        work(column(d - 1) + x)

    def next_across(d):
        arrive_across(d)
        work(column(d - 1) + 1 - x)

    arrive_across(0)
    arrive_column(1)
    loop(1, n, table_wait)
    work(column(0) + 1 - x)
    loop(2, columns, next_column)
    arrive_across(1)
    work(column(columns - 1) + x)
    loop(2, columns, next_across)
    work(column(columns - 1) + 1 - x)

    both = acc[...].astype(jnp.bfloat16)
    products = contract(all_feats[me], both, 0, 0)
    for c in range(n):
        piece = products[c * share : (c + 1) * share]
        terms[c] = piece
        outgoing[c] = piece.astype(jnp.bfloat16)

    def weight_copy(d):
        target = lax.rem(me + d, n)
        return push(
            outgoing.at[target], arrived.at[n - d], w_send.at[d], w_recv.at[n - d], {"img": target}
        )

    loop(1, n, lambda d: weight_copy(d).start())
    for c in range(2):
        part = slice(c * width, (c + 1) * width)
        term[c] = contract(both[:, :width], w_qk[part], 1, 1) + contract(
            both[:, width:], w_v[part], 1, 1
        )
    swap = push(term.at[1 - sub], term_in, s_send.at[0], s_recv.at[0], partner)
    swap.start()
    swap.wait_recv()
    grad_feats[0] = (term[sub] + term_in[...]).astype(grad_feats.dtype)

    total = terms[me]
    loop(1, n, lambda d: weight_copy(d).wait_recv())
    for d in range(1, n):
        total = total + arrived[d].astype(jnp.float32)
    grad_weights[0] = total[:, :width]
    grad_weights[1] = total[:, width:]

    swap.wait_send()
    loop(1, n, lambda d: weight_copy(d).wait_send())
    loop(1, n, lambda d: table_copy(d).wait_send())
    own_feats(xf_send.at[0], across).wait_send()
    own_grad(xg_send.at[0], across).wait_send()

    def sent_column(d):
        own_feats(zf_send.at[d], column_target(d)).wait_send()
        own_grad(zg_send.at[d], column_target(d)).wait_send()
        feats_x(column(d) + x, d).wait_send()
        grad_x(column(d) + x, d).wait_send()

    loop(1, columns, sent_column)
    loop(1, n, lambda d: core(lax.rem(me + d, n), mine).wait_send())


def local(feats, grad_msg, w_qk, w_v, pair_slots, counts):
    n = lax.axis_size("img")
    rows, depth = feats.shape[1:]
    width = w_qk.shape[1]
    share = depth // n
    low, full = jnp.bfloat16, jnp.float32
    vmem = pltpu.VMEM
    dma = pltpu.SemaphoreType.DMA
    return pl.pallas_call(
        functools.partial(kernel, n),
        out_shape=(
            jax.ShapeDtypeStruct((1, rows, width), low),
            jax.ShapeDtypeStruct((2, share, width), full),
        ),
        in_specs=[HBM] * 4 + [SMEM] * 2,
        out_specs=(VMEM,) * 2,
        scratch_shapes=[
            vmem((n, rows, depth), low),
            vmem((n, rows, width), low),
            vmem((n, 2, LANES), jnp.int32),
            vmem((depth, width), low),
            vmem((depth, width), low),
            vmem((rows, 2 * width), full),
            vmem((n, share, 2 * width), full),
            vmem((n, share, 2 * width), low),
            vmem((n, share, 2 * width), low),
            vmem((2, rows, width), full),
            vmem((rows, width), full),
            dma((4,)),
            dma((n // 2,)), dma((n // 2,)), dma((n // 2,)), dma((n // 2,)),
            dma((n,)), dma((n,)), dma((n,)), dma((n,)), dma((n,)), dma((n,)),
            dma((n,)), dma((n,)), dma((1,)), dma((1,)),
        ],
        compiler_params=pltpu.CompilerParams(
            collective_id=0, has_side_effects=True, vmem_limit_bytes=64 * 1024 * 1024
        ),
        name="backward",
    )(feats, grad_msg, w_qk, w_v, jnp.transpose(pair_slots, (0, 2, 1)), counts)


def solution(mesh):
    in_specs = (
        P(("groups", "img"), None, None),
        P(("groups", "img"), None, "sub"),
        P(None, "sub"),
        P(None, "sub"),
        P(("groups", "img"), None, None),
        P(("groups", "img")),
    )
    out_specs = (P(("groups", "img"), None, "sub"), P("groups", "img", "sub"))
    return jax.shard_map(local, mesh=mesh, in_specs=in_specs, out_specs=out_specs, check_vma=False)
```

```python
import functools

import jax
import jax.numpy as jnp
from jax import lax
from jax.experimental import pallas as pl
from jax.experimental.pallas import tpu as pltpu
from jax.sharding import PartitionSpec as P

HEAD_DIM = 64
NEG_FILL = -1e30
LANES = 128
MESH = pl.DeviceIdType.MESH
HBM = pl.BlockSpec(memory_space=pltpu.HBM)
VMEM = pl.BlockSpec(memory_space=pltpu.VMEM)
SMEM = pl.BlockSpec(memory_space=pltpu.SMEM)


def contract(left, right, left_dim, right_dim):
    return lax.dot_general(
        left, right, (((left_dim,), (right_dim,)), ((), ())), preferred_element_type=jnp.float32
    )


def loop(low, high, body):
    if high - low <= 8:
        for d in range(low, high):
            body(d)
    else:

        def step(d, carry):
            body(d)
            return carry

        lax.fori_loop(low, high, step, 0)


def kernel(
    n, feats, grad, w_qk_in, w_v_in, pairs, counts, grad_feats, grad_weights,
    all_feats, all_grad, table, weights, acc, terms, outgoing, arrived, term, term_in,
    local_sem, zf_send, zg_send, xf_send, xg_send, c_send, t_send, f_recv, g_recv, c_recv, t_recv,
    w_send, w_recv, s_send, s_recv,
):
    me = lax.axis_index("img")
    sub = lax.axis_index("sub")
    columns = n // 2
    z, x = me // 2, lax.rem(me, 2)
    rows = feats.shape[1]
    half = rows // 2
    width = w_qk_in.shape[1]
    heads = width // HEAD_DIM
    scale = HEAD_DIM ** (-0.5)
    share = terms.shape[1]
    mine = pl.ds(pl.multiple_of(sub * half, half), half)
    other = pl.ds(pl.multiple_of((1 - sub) * half, half), half)
    across = {"img": z * 2 + 1 - x}
    partner = {"sub": 1 - sub}

    barrier = pltpu.get_barrier_semaphore()
    loop(1, n, lambda d: pl.semaphore_signal(
        barrier, inc=1, device_id={"img": lax.rem(me + d, n)}, device_id_type=MESH
    ))
    pl.semaphore_signal(barrier, inc=1, device_id=partner, device_id_type=MESH)

    own = [
        pltpu.make_async_copy(feats.at[0], all_feats.at[me], local_sem.at[0]),
        pltpu.make_async_copy(w_qk_in, weights.at[:, pl.ds(0, width)], local_sem.at[1]),
        pltpu.make_async_copy(w_v_in, weights.at[:, pl.ds(width, width)], local_sem.at[2]),
        pltpu.make_async_copy(grad.at[0], all_grad.at[me], local_sem.at[3]),
    ]
    for copy in own:
        copy.start()

    lane = lax.broadcasted_iota(jnp.int32, (1, LANES), 1)
    codes = jnp.full((1, LANES), -1, jnp.int32)
    for k in range(pairs.shape[2]):
        left, right = pairs[0, 0, k], pairs[0, 1, k]
        codes = jnp.where(lane == k, jnp.where(left >= 0, left * n + right, -1), codes)
    table[me] = jnp.concatenate([codes, jnp.full((1, LANES), counts[0], jnp.int32)], axis=0)
    for copy in own:
        copy.wait()
    pl.semaphore_wait(barrier, n)

    def push(src, dst, send, recv, device):
        return pltpu.make_async_remote_copy(
            src_ref=src, dst_ref=dst, send_sem=send, recv_sem=recv,
            device_id=device, device_id_type=MESH,
        )

    def column(d):
        meets, bit = z, 1
        while bit < columns:
            meets = meets + (d // bit % 2) * (bit - 2 * bit * (z // bit % 2))
            bit *= 2
        return meets * 2

    def feats_x(block, d):
        return push(
            all_feats.at[block, mine], all_feats.at[block, mine], xf_send.at[d], f_recv.at[block], across
        )

    def grad_x(block, d):
        return push(all_grad.at[block], all_grad.at[block], xg_send.at[d], g_recv.at[block], across)

    def own_feats(send, device):
        return push(all_feats.at[me, mine], all_feats.at[me, mine], send, f_recv.at[me], device)

    def own_grad(send, device):
        return push(all_grad.at[me], all_grad.at[me], send, g_recv.at[me], device)

    def column_target(d):
        return {"img": column(d) + x}

    def core(block, half_rows):
        return push(
            all_feats.at[block, half_rows], all_feats.at[block, half_rows], c_send.at[block],
            c_recv.at[block], partner,
        )

    def table_copy(d):
        return push(
            table.at[me], table.at[me], t_send.at[d], t_recv.at[me], {"img": lax.rem(me + d, n)}
        )

    def table_wait(d):
        block = lax.rem(me + d, n)
        push(
            table.at[block], table.at[block], t_send.at[d], t_recv.at[block], {"img": block}
        ).wait_recv()

    loop(1, n, lambda d: table_copy(d).start())
    own_feats(xf_send.at[0], across).start()
    own_grad(xg_send.at[0], across).start()

    def send_column(d):
        own_feats(zf_send.at[d], column_target(d)).start()
        own_grad(zg_send.at[d], column_target(d)).start()

    loop(1, columns, lambda d: send_column(d))

    def arrive_column(d):
        block = column(d) + x
        feats_x(block, d).wait_recv()
        feats_x(block, d).start()
        core(block, mine).start()
        grad_x(block, d).wait_recv()
        grad_x(block, d).start()

    def arrive_across(d):
        block = column(d) + 1 - x
        feats_x(block, d).wait_recv()
        core(block, mine).start()
        grad_x(block, d).wait_recv()

    row_ids = lax.broadcasted_iota(jnp.int32, (rows, width), 0)

    def project(which):
        projected = contract(all_feats[which], weights[...], 1, 0).astype(jnp.bfloat16)
        q, v = projected[:, :width], projected[:, width:]
        count = table[which, 1:2, :]
        g = jnp.where(row_ids < count, all_grad[which], jnp.zeros((), jnp.bfloat16))
        return q, v, g, count

    def stack(part):
        head = lax.broadcasted_iota(jnp.int32, part.shape, 1) // HEAD_DIM
        zero = jnp.zeros((), part.dtype)
        return jnp.concatenate([jnp.where(head == h, part, zero) for h in range(heads)], axis=0)

    q_own, v_own, g_own, count_own = project(me)
    wide = (rows, heads * rows)
    row_live = lax.broadcasted_iota(jnp.int32, wide, 0) < jnp.concatenate([count_own] * heads, axis=1)
    acc[...] = jnp.zeros_like(acc)

    def work(peer):
        core(peer, other).wait_recv()
        q_peer, v_peer, g_peer, count_peer = project(peer)
        q_peer, v_peer, g_peer = stack(q_peer), stack(v_peer), stack(g_peer)
        listed = table[:, 0, :]
        hits = (listed == me * n + peer) | (listed == peer * n + me)
        times = jnp.sum(hits.astype(jnp.float32), keepdims=True)
        scores = contract(q_own, q_peer, 1, 1) * scale
        drow = contract(g_own, v_peer, 1, 1)
        dcol = contract(v_own, g_peer, 1, 1)
        masked = jnp.where(row_live, scores, NEG_FILL)
        e = jnp.exp(masked - jnp.max(masked, axis=0, keepdims=True))
        col = e * (1.0 / jnp.sum(e, axis=0, keepdims=True))
        dcol = col * (dcol - jnp.sum(dcol * col, axis=0, keepdims=True))
        col_live = lax.broadcasted_iota(jnp.int32, (rows, rows), 1) < count_peer
        pieces = []
        for h in range(heads):
            part = slice(h * rows, (h + 1) * rows)
            masked = jnp.where(col_live, scores[:, part], NEG_FILL)
            e = jnp.exp(masked - jnp.max(masked, axis=1, keepdims=True))
            row = e * (1.0 / jnp.sum(e, axis=1, keepdims=True))
            d = drow[:, part]
            d = row * (d - jnp.sum(d * row, axis=1, keepdims=True))
            pieces.append(((d + dcol[:, part]) * scale).astype(jnp.bfloat16))
        dscore = jnp.concatenate(pieces, axis=1)
        acc[:, :width] += times * contract(dscore, q_peer, 1, 0)
        acc[:, width:] += times * contract(col.astype(jnp.bfloat16), g_peer, 1, 0)

    def next_column(d):
        arrive_column(d)
        work(column(d - 1) + x)

    def next_across(d):
        arrive_across(d)
        work(column(d - 1) + 1 - x)

    arrive_across(0)
    arrive_column(1)
    loop(1, n, table_wait)
    work(column(0) + 1 - x)
    loop(2, columns, next_column)
    arrive_across(1)
    work(column(columns - 1) + x)
    loop(2, columns, next_across)
    work(column(columns - 1) + 1 - x)

    both = acc[...].astype(jnp.bfloat16)
    products = contract(all_feats[me], both, 0, 0)
    for c in range(n):
        piece = products[c * share : (c + 1) * share]
        terms[c] = piece
        outgoing[c] = piece.astype(jnp.bfloat16)

    def weight_copy(d):
        target = lax.rem(me + d, n)
        return push(
            outgoing.at[target], arrived.at[n - d], w_send.at[d], w_recv.at[n - d], {"img": target}
        )

    loop(1, n, lambda d: weight_copy(d).start())
    for c in range(2):
        term[c] = contract(both, weights[c * width : (c + 1) * width], 1, 1)
    swap = push(term.at[1 - sub], term_in, s_send.at[0], s_recv.at[0], partner)
    swap.start()
    loop(1, n, lambda d: table_copy(d).wait_send())
    own_feats(xf_send.at[0], across).wait_send()
    own_grad(xg_send.at[0], across).wait_send()

    def sent_column(d):
        own_feats(zf_send.at[d], column_target(d)).wait_send()
        own_grad(zg_send.at[d], column_target(d)).wait_send()
        feats_x(column(d) + x, d).wait_send()
        grad_x(column(d) + x, d).wait_send()

    loop(1, columns, sent_column)
    loop(1, n, lambda d: core(lax.rem(me + d, n), mine).wait_send())
    swap.wait_recv()
    grad_feats[0] = (term[sub] + term_in[...]).astype(grad_feats.dtype)

    total = terms[me]
    loop(1, n, lambda d: weight_copy(d).wait_recv())
    for d in range(1, n):
        total = total + arrived[d].astype(jnp.float32)
    grad_weights[0] = total[:, :width]
    grad_weights[1] = total[:, width:]

    swap.wait_send()
    loop(1, n, lambda d: weight_copy(d).wait_send())


def local(feats, grad_msg, w_qk, w_v, pair_slots, counts):
    n = lax.axis_size("img")
    rows, depth = feats.shape[1:]
    width = w_qk.shape[1]
    share = depth // n
    low, full = jnp.bfloat16, jnp.float32
    vmem = pltpu.VMEM
    dma = pltpu.SemaphoreType.DMA
    return pl.pallas_call(
        functools.partial(kernel, n),
        out_shape=(
            jax.ShapeDtypeStruct((1, rows, width), low),
            jax.ShapeDtypeStruct((2, share, width), full),
        ),
        in_specs=[HBM] * 4 + [SMEM] * 2,
        out_specs=(VMEM,) * 2,
        scratch_shapes=[
            vmem((n, rows, depth), low),
            vmem((n, rows, width), low),
            vmem((n, 2, LANES), jnp.int32),
            vmem((depth, 2 * width), low),
            vmem((rows, 2 * width), full),
            vmem((n, share, 2 * width), full),
            vmem((n, share, 2 * width), low),
            vmem((n, share, 2 * width), low),
            vmem((2, rows, width), full),
            vmem((rows, width), full),
            dma((4,)),
            dma((n // 2,)), dma((n // 2,)), dma((n // 2,)), dma((n // 2,)),
            dma((n,)), dma((n,)), dma((n,)), dma((n,)), dma((n,)), dma((n,)),
            dma((n,)), dma((n,)), dma((1,)), dma((1,)),
        ],
        compiler_params=pltpu.CompilerParams(
            collective_id=0, has_side_effects=True, vmem_limit_bytes=64 * 1024 * 1024
        ),
        name="backward",
    )(feats, grad_msg, w_qk, w_v, jnp.transpose(pair_slots, (0, 2, 1)), counts)


def solution(mesh):
    in_specs = (
        P(("groups", "img"), None, None),
        P(("groups", "img"), None, "sub"),
        P(None, "sub"),
        P(None, "sub"),
        P(("groups", "img"), None, None),
        P(("groups", "img")),
    )
    out_specs = (P(("groups", "img"), None, "sub"), P("groups", "img", "sub"))
    return jax.shard_map(local, mesh=mesh, in_specs=in_specs, out_specs=out_specs, check_vma=False)
```

```python
import functools

import jax
import jax.numpy as jnp
from jax import lax
from jax.experimental import pallas as pl
from jax.experimental.pallas import tpu as pltpu
from jax.sharding import PartitionSpec as P

HEAD_DIM = 64
NEG_FILL = -1e30
LANES = 128
MESH = pl.DeviceIdType.MESH
HBM = pl.BlockSpec(memory_space=pltpu.HBM)
VMEM = pl.BlockSpec(memory_space=pltpu.VMEM)
SMEM = pl.BlockSpec(memory_space=pltpu.SMEM)


def contract(left, right, left_dim, right_dim):
    return lax.dot_general(
        left, right, (((left_dim,), (right_dim,)), ((), ())), preferred_element_type=jnp.float32
    )


def loop(low, high, body):
    if high - low <= 8:
        for d in range(low, high):
            body(d)
    else:

        def step(d, carry):
            body(d)
            return carry

        lax.fori_loop(low, high, step, 0)


def kernel(
    n, feats, grad, w_qk_in, w_v_in, pairs, counts, grad_feats, grad_weights,
    all_feats, all_grad, table, weights, acc, terms, outgoing, arrived, term, term_in,
    local_sem, zf_send, zg_send, xf_send, xg_send, c_send, t_send, f_recv, g_recv, c_recv, t_recv,
    w_send, w_recv, s_send, s_recv,
):
    me = lax.axis_index("img")
    sub = lax.axis_index("sub")
    columns = n // 2
    z, x = me // 2, lax.rem(me, 2)
    rows = feats.shape[1]
    half = rows // 2
    width = w_qk_in.shape[1]
    heads = width // HEAD_DIM
    scale = HEAD_DIM ** (-0.5)
    share = terms.shape[1]
    mine = pl.ds(pl.multiple_of(sub * half, half), half)
    other = pl.ds(pl.multiple_of((1 - sub) * half, half), half)
    across = {"img": z * 2 + 1 - x}
    partner = {"sub": 1 - sub}

    barrier = pltpu.get_barrier_semaphore()
    loop(1, n, lambda d: pl.semaphore_signal(
        barrier, inc=1, device_id={"img": lax.rem(me + d, n)}, device_id_type=MESH
    ))
    pl.semaphore_signal(barrier, inc=1, device_id=partner, device_id_type=MESH)

    own = [
        pltpu.make_async_copy(feats.at[0], all_feats.at[me], local_sem.at[0]),
        pltpu.make_async_copy(w_qk_in, weights.at[:, pl.ds(0, width)], local_sem.at[1]),
        pltpu.make_async_copy(w_v_in, weights.at[:, pl.ds(width, width)], local_sem.at[2]),
        pltpu.make_async_copy(grad.at[0], all_grad.at[me], local_sem.at[3]),
    ]
    for copy in own:
        copy.start()

    lane = lax.broadcasted_iota(jnp.int32, (1, LANES), 1)
    codes = jnp.full((1, LANES), -1, jnp.int32)
    for k in range(pairs.shape[2]):
        left, right = pairs[0, 0, k], pairs[0, 1, k]
        codes = jnp.where(lane == k, jnp.where(left >= 0, left * n + right, -1), codes)
    table[me] = jnp.concatenate([codes, jnp.full((1, LANES), counts[0], jnp.int32)], axis=0)
    for copy in own:
        copy.wait()
    pl.semaphore_wait(barrier, n)

    def push(src, dst, send, recv, device):
        return pltpu.make_async_remote_copy(
            src_ref=src, dst_ref=dst, send_sem=send, recv_sem=recv,
            device_id=device, device_id_type=MESH,
        )

    def column(d):
        meets, bit = z, 1
        while bit < columns:
            meets = meets + (d // bit % 2) * (bit - 2 * bit * (z // bit % 2))
            bit *= 2
        return meets * 2

    def feats_x(block, d):
        return push(
            all_feats.at[block, mine], all_feats.at[block, mine], xf_send.at[d], f_recv.at[block], across
        )

    def grad_x(block, d):
        return push(all_grad.at[block], all_grad.at[block], xg_send.at[d], g_recv.at[block], across)

    def own_feats(send, device):
        return push(all_feats.at[me, mine], all_feats.at[me, mine], send, f_recv.at[me], device)

    def own_grad(send, device):
        return push(all_grad.at[me], all_grad.at[me], send, g_recv.at[me], device)

    def column_target(d):
        return {"img": column(d) + x}

    def core(block, half_rows):
        return push(
            all_feats.at[block, half_rows], all_feats.at[block, half_rows], c_send.at[block],
            c_recv.at[block], partner,
        )

    def table_copy(d):
        return push(
            table.at[me], table.at[me], t_send.at[d], t_recv.at[me], {"img": lax.rem(me + d, n)}
        )

    def table_wait(d):
        block = lax.rem(me + d, n)
        push(
            table.at[block], table.at[block], t_send.at[d], t_recv.at[block], {"img": block}
        ).wait_recv()

    loop(1, n, lambda d: table_copy(d).start())

    def send_column(d):
        own_feats(zf_send.at[d], column_target(d)).start()
        own_grad(zg_send.at[d], column_target(d)).start()

    loop(1, columns, lambda d: send_column(d))
    own_feats(xf_send.at[0], across).start()
    own_grad(xg_send.at[0], across).start()

    def arrive_column(d):
        block = column(d) + x
        feats_x(block, d).wait_recv()
        feats_x(block, d).start()
        core(block, mine).start()
        grad_x(block, d).wait_recv()
        grad_x(block, d).start()

    def arrive_across(d):
        block = column(d) + 1 - x
        feats_x(block, d).wait_recv()
        core(block, mine).start()
        grad_x(block, d).wait_recv()

    row_ids = lax.broadcasted_iota(jnp.int32, (rows, width), 0)

    def project(which):
        projected = contract(all_feats[which], weights[...], 1, 0).astype(jnp.bfloat16)
        q, v = projected[:, :width], projected[:, width:]
        count = table[which, 1:2, :]
        g = jnp.where(row_ids < count, all_grad[which], jnp.zeros((), jnp.bfloat16))
        return q, v, g, count

    def stack(part):
        head = lax.broadcasted_iota(jnp.int32, part.shape, 1) // HEAD_DIM
        zero = jnp.zeros((), part.dtype)
        return jnp.concatenate([jnp.where(head == h, part, zero) for h in range(heads)], axis=0)

    q_own, v_own, g_own, count_own = project(me)
    wide = (rows, heads * rows)
    row_live = lax.broadcasted_iota(jnp.int32, wide, 0) < jnp.concatenate([count_own] * heads, axis=1)
    acc[...] = jnp.zeros_like(acc)

    def work(peer):
        core(peer, other).wait_recv()
        q_peer, v_peer, g_peer, count_peer = project(peer)
        q_peer, v_peer, g_peer = stack(q_peer), stack(v_peer), stack(g_peer)
        listed = table[:, 0, :]
        hits = (listed == me * n + peer) | (listed == peer * n + me)
        times = jnp.sum(hits.astype(jnp.float32), keepdims=True)
        scores = contract(q_own, q_peer, 1, 1) * scale
        drow = contract(g_own, v_peer, 1, 1)
        dcol = contract(v_own, g_peer, 1, 1)
        masked = jnp.where(row_live, scores, NEG_FILL)
        e = jnp.exp(masked - jnp.max(masked, axis=0, keepdims=True))
        col = e * (1.0 / jnp.sum(e, axis=0, keepdims=True))
        dcol = col * (dcol - jnp.sum(dcol * col, axis=0, keepdims=True))
        col_live = lax.broadcasted_iota(jnp.int32, (rows, rows), 1) < count_peer
        pieces = []
        for h in range(heads):
            part = slice(h * rows, (h + 1) * rows)
            masked = jnp.where(col_live, scores[:, part], NEG_FILL)
            e = jnp.exp(masked - jnp.max(masked, axis=1, keepdims=True))
            row = e * (1.0 / jnp.sum(e, axis=1, keepdims=True))
            d = drow[:, part]
            d = row * (d - jnp.sum(d * row, axis=1, keepdims=True))
            pieces.append(((d + dcol[:, part]) * scale).astype(jnp.bfloat16))
        dscore = jnp.concatenate(pieces, axis=1)
        acc[:, :width] += times * contract(dscore, q_peer, 1, 0)
        acc[:, width:] += times * contract(col.astype(jnp.bfloat16), g_peer, 1, 0)

    def next_column(d):
        arrive_column(d)
        work(column(d - 1) + x)

    def next_across(d):
        arrive_across(d)
        work(column(d - 1) + 1 - x)

    arrive_across(0)
    arrive_column(1)
    loop(1, n, table_wait)
    work(column(0) + 1 - x)
    loop(2, columns, next_column)
    arrive_across(1)
    work(column(columns - 1) + x)
    loop(2, columns, next_across)
    work(column(columns - 1) + 1 - x)

    both = acc[...].astype(jnp.bfloat16)
    products = contract(all_feats[me], both, 0, 0)
    for c in range(n):
        piece = products[c * share : (c + 1) * share]
        terms[c] = piece
        outgoing[c] = piece.astype(jnp.bfloat16)

    def weight_copy(d):
        target = lax.rem(me + d, n)
        return push(
            outgoing.at[target], arrived.at[n - d], w_send.at[d], w_recv.at[n - d], {"img": target}
        )

    loop(1, n, lambda d: weight_copy(d).start())
    for c in range(2):
        term[c] = contract(both, weights[c * width : (c + 1) * width], 1, 1)
    swap = push(term.at[1 - sub], term_in, s_send.at[0], s_recv.at[0], partner)
    swap.start()
    loop(1, n, lambda d: table_copy(d).wait_send())
    own_feats(xf_send.at[0], across).wait_send()
    own_grad(xg_send.at[0], across).wait_send()

    def sent_column(d):
        own_feats(zf_send.at[d], column_target(d)).wait_send()
        own_grad(zg_send.at[d], column_target(d)).wait_send()
        feats_x(column(d) + x, d).wait_send()
        grad_x(column(d) + x, d).wait_send()

    loop(1, columns, sent_column)
    loop(1, n, lambda d: core(lax.rem(me + d, n), mine).wait_send())
    swap.wait_recv()
    grad_feats[0] = (term[sub] + term_in[...]).astype(grad_feats.dtype)

    total = terms[me]
    loop(1, n, lambda d: weight_copy(d).wait_recv())
    for d in range(1, n):
        total = total + arrived[d].astype(jnp.float32)
    grad_weights[0] = total[:, :width]
    grad_weights[1] = total[:, width:]

    swap.wait_send()
    loop(1, n, lambda d: weight_copy(d).wait_send())


def local(feats, grad_msg, w_qk, w_v, pair_slots, counts):
    n = lax.axis_size("img")
    rows, depth = feats.shape[1:]
    width = w_qk.shape[1]
    share = depth // n
    low, full = jnp.bfloat16, jnp.float32
    vmem = pltpu.VMEM
    dma = pltpu.SemaphoreType.DMA
    return pl.pallas_call(
        functools.partial(kernel, n),
        out_shape=(
            jax.ShapeDtypeStruct((1, rows, width), low),
            jax.ShapeDtypeStruct((2, share, width), full),
        ),
        in_specs=[HBM] * 4 + [SMEM] * 2,
        out_specs=(VMEM,) * 2,
        scratch_shapes=[
            vmem((n, rows, depth), low),
            vmem((n, rows, width), low),
            vmem((n, 2, LANES), jnp.int32),
            vmem((depth, 2 * width), low),
            vmem((rows, 2 * width), full),
            vmem((n, share, 2 * width), full),
            vmem((n, share, 2 * width), low),
            vmem((n, share, 2 * width), low),
            vmem((2, rows, width), full),
            vmem((rows, width), full),
            dma((4,)),
            dma((n // 2,)), dma((n // 2,)), dma((n // 2,)), dma((n // 2,)),
            dma((n,)), dma((n,)), dma((n,)), dma((n,)), dma((n,)), dma((n,)),
            dma((n,)), dma((n,)), dma((1,)), dma((1,)),
        ],
        compiler_params=pltpu.CompilerParams(
            collective_id=0, has_side_effects=True, vmem_limit_bytes=64 * 1024 * 1024
        ),
        name="backward",
    )(feats, grad_msg, w_qk, w_v, jnp.transpose(pair_slots, (0, 2, 1)), counts)


def solution(mesh):
    in_specs = (
        P(("groups", "img"), None, None),
        P(("groups", "img"), None, "sub"),
        P(None, "sub"),
        P(None, "sub"),
        P(("groups", "img"), None, None),
        P(("groups", "img")),
    )
    out_specs = (P(("groups", "img"), None, "sub"), P("groups", "img", "sub"))
    return jax.shard_map(local, mesh=mesh, in_specs=in_specs, out_specs=out_specs, check_vma=False)
```
